32 devices in a mesh: pts: 4 (over y, x), lmk: 8 (over z, core).
Axes of the slice: x: 2, y: 2, z: 4, core: 2. Of those that a mesh axis runs over, the one named last changes fastest.
Arguments:
- points: float32 [16384, 384], P('pts'), may hold values from -8 to 8
- labels: int32 [16384], P('pts'), may hold values from 0 to 127
- landmarks: float32 [16384, 384], P('lmk'), may hold values from -8 to 8
- coefficients: float32 [16384, 128], P('lmk'), may hold values from -4 to 4
Outputs:
- gradient: float32 [16384, 128], P('lmk')
The draws below stay inside these ranges and needn't reach their ends.
All inputs are finite; a program needn't handle non-finite values.
Results may differ from the reference program's by a relative error of at most 0.0003.
Values sent between devices are 32-bit elements; how exact they have to be, the bound alone decides.
A program may use at most 128 MiB of HBM per device.

```python
import jax
import jax.numpy as jnp
from jax import lax

F = 384
K = 128
NP_DEV = 4096
NPTS = 16384
M = 16384
N_PTS = 4


cluster_count = 64


latent_rank = 4


latent_spread = 0.7071


noise_level = 0.5


value_limit = 8.0


def cluster_layout(key):
    maps = jax.random.truncated_normal(jax.random.fold_in(key, 8), -3.0, 3.0, (cluster_count, latent_rank, F), jnp.float32) * latent_spread
    centres = jax.random.truncated_normal(jax.random.fold_in(key, 7), -3.0, 3.0, (cluster_count, F), jnp.float32)
    return (centres, maps)


def point_members(key):
    return jax.random.randint(jax.random.fold_in(key, 11), (NPTS,), 0, cluster_count)


def landmark_members(key):
    return jax.random.randint(jax.random.fold_in(key, 13), (M,), 0, cluster_count)


def place_members(key, member, salt):
    high = lax.Precision.HIGHEST
    centres, maps = cluster_layout(key)
    count = member.shape[0]
    latent = jax.random.truncated_normal(jax.random.fold_in(key, salt), -3.0, 3.0, (count, latent_rank), jnp.float32)
    noise = jax.random.truncated_normal(jax.random.fold_in(key, salt + 1), -3.0, 3.0, (count, F), jnp.float32) * noise_level
    selector = (member[:, None] == jnp.arange(cluster_count, dtype=jnp.int32)[None, :]).astype(jnp.float32)
    spread_in = (selector[:, :, None] * latent[:, None, :]).reshape(count, cluster_count * latent_rank)
    spread = jnp.dot(spread_in, maps.reshape(cluster_count * latent_rank, F), precision=high)
    base = jnp.dot(selector, centres, precision=high)
    values = base + spread + noise
    return jnp.clip(values, -value_limit, value_limit)


def draw_points(key, part):
    return place_members(key, point_members(key), 21)


def draw_landmarks(key, part):
    return place_members(key, landmark_members(key), 31)


def draw_labels(key, part):
    member = point_members(key)
    class_of = jax.random.randint(jax.random.fold_in(key, 12), (cluster_count,), 0, K)
    mixing = jax.random.randint(jax.random.fold_in(key, 14), (NPTS,), 0, 4)
    others = jax.random.randint(jax.random.fold_in(key, 15), (NPTS,), 0, K)
    return jnp.where(mixing > 0, class_of[member], others).astype(jnp.int32)


def steps_of(key, extent, pieces, low, high):
    gain, own = 1.0, jax.random.fold_in(key, 6)
    for position, shards_of in pieces:
        draws = jnp.exp(jax.random.uniform(jax.random.fold_in(own, position), (shards_of,), jnp.float32, low / len(pieces), high / len(pieces)))
        gain = gain * jnp.repeat(draws, extent[position] // shards_of).reshape([-1 if axis == position else 1 for axis in range(len(extent))])
    return gain


def gaussian(rng, extent, deviation, limit, shards=(), held_as=jnp.bfloat16):
    values = deviation * jax.random.normal(rng, extent, jnp.float32)
    if shards:
        values = values * steps_of(rng, extent, shards, -0.22, 0.18)
    return jnp.clip(values, -limit, limit).astype(held_as)


def setup_inputs(seed: int = 0) -> dict:
    key_of = jax.random.split(jax.random.key(seed), 5)
    points = draw_points(jax.random.fold_in(key_of[4], 71), 0)
    labels = draw_labels(jax.random.fold_in(key_of[4], 71), 0)
    landmarks = draw_landmarks(jax.random.fold_in(key_of[4], 71), 0)
    coefficients = gaussian(key_of[3], (M, K), (max(1, M // 8192)) ** -0.5, 4.0, ((0, 8),), jnp.float32)
    return {"points": points, "labels": labels, "landmarks": landmarks, "coefficients": coefficients}


LOSS_SCALE = 8192.0
RIDGE = 0.5


def reference(points, labels, landmarks, coefficients):
    high = lax.Precision.HIGHEST
    feats = points.shape[1]
    total_points = points.shape[0]
    lnorm = jnp.sum(landmarks * landmarks, axis=1)
    blocks_pts = points.reshape(N_PTS, NP_DEV, feats)
    blocks_lab = labels.reshape(N_PTS, NP_DEV)
    classes = coefficients.shape[1]

    def step(carry, block):
        pblock, lblock = block
        pnorm = jnp.sum(pblock * pblock, axis=1)
        cross = jnp.dot(pblock, landmarks.T, precision=high, preferred_element_type=jnp.float32)
        kernel = jnp.exp(-(pnorm[:, None] + lnorm[None, :] - 2.0 * cross) / feats)
        logits = jnp.dot(kernel, coefficients, precision=high, preferred_element_type=jnp.float32)
        expo = jnp.exp(logits)
        onehot = (lblock[:, None] == jnp.arange(classes, dtype=jnp.int32)[None, :]).astype(jnp.float32)
        resid = expo / jnp.sum(expo, axis=1, keepdims=True) - onehot
        term = lax.dot_general(kernel, resid, (((0,), (0,)), ((), ())), precision=high, preferred_element_type=jnp.float32)
        return carry + term, None

    start = jnp.zeros(coefficients.shape, jnp.float32)
    summed, unused = lax.scan(step, start, (blocks_pts, blocks_lab))
    return summed * (LOSS_SCALE / total_points) + RIDGE * coefficients
```

```python
import functools

import jax
import jax.numpy as jnp
from jax import lax
from jax.experimental import pallas as pl
from jax.experimental.pallas import tpu as pltpu
from jax.sharding import PartitionSpec as P

LOSS_SCALE = 8192.0
RIDGE = 0.5
LOG2E = 1.4426950408889634
BF = jnp.bfloat16
F32 = jnp.float32


def halves(x):
    hi = x.astype(BF)
    return hi, (x - hi.astype(F32)).astype(BF)


def dot(a, b):
    return jnp.dot(a, b, preferred_element_type=F32)


def dot_nt(a, b):
    return lax.dot_general(a, b, (((1,), (1,)), ((), ())), preferred_element_type=F32)


def extra_columns(norm, first):
    n1 = norm.astype(BF).astype(F32)
    n2 = (norm - n1).astype(BF).astype(F32)
    n3 = ((norm - n1) - n2).astype(BF).astype(F32)
    lane = lax.broadcasted_iota(jnp.int32, (norm.shape[0], 128), 1)
    ones = jnp.where((lane >= 3 - first) & (lane < 6 - first), 1.0, 0.0)
    ext = jnp.where(lane == first, n1, ones)
    ext = jnp.where(lane == first + 1, n2, ext)
    return jnp.where(lane == first + 2, n3, ext).astype(BF)


def body(cfg, pts_ref, lab_ref, lmk_ref, coef_ref, out_ref,
         ls, cc, ps, kh, kl, logit, prob, recv, acc, grecv,
         send_sem, recv_sem, gsend, grecv_sem):
    rows, tile, npts, nlmk, scale = cfg
    n, feats = pts_ref.shape
    m, classes = coef_ref.shape
    chunks = n // rows
    lbits, pbits = nlmk.bit_length() - 1, npts.bit_length() - 1
    stages = 2 * lbits
    my_l, my_p = lax.axis_index("lmk"), lax.axis_index("pts")

    barrier = pltpu.get_barrier_semaphore()
    for b in range(lbits):
        pl.semaphore_signal(barrier, inc=1, device_id={"lmk": my_l ^ (1 << b)},
                            device_id_type=pl.DeviceIdType.MESH)
    for b in range(pbits):
        pl.semaphore_signal(barrier, inc=1, device_id={"pts": my_p ^ (1 << b)},
                            device_id_type=pl.DeviceIdType.MESH)
    pl.semaphore_wait(barrier, lbits + pbits)

    def split_landmarks(i, _):
        r = pl.ds(pl.multiple_of(i * tile, tile), tile)
        x = lmk_ref[r, :]
        hi, lo = halves(x * (2.0 * LOG2E / feats))
        ls[r, :feats] = hi
        ls[r, feats:2 * feats] = hi
        ls[r, 2 * feats:3 * feats] = lo
        norm = jnp.sum(x * x, axis=1, keepdims=True) * (-LOG2E / feats)
        ls[r, 3 * feats:] = extra_columns(norm, 3)
        hi, lo = halves(coef_ref[r, :])
        cc[r, :classes] = hi
        cc[r, classes:] = lo
        return 0

    lax.fori_loop(0, m // tile, split_landmarks, 0)
    acc[...] = jnp.zeros_like(acc)

    def region(me, bits, total):
        offset, size = 0, total
        for b in bits:
            size //= 2
            offset = offset + ((me >> b) & 1) * size
        return offset, size

    order = list(range(lbits))
    recv_base = [rows - (rows >> s) for s in range(lbits)]

    def exchange(s, chunk):
        base = chunk * rows
        if s < lbits:
            b = order[s]
            at, size = region(my_l, order[:s], rows)
            size //= 2
            other = 1 - ((my_l >> b) & 1)
            src = logit.at[pl.ds(pl.multiple_of(base + at + other * size, 8), size), :]
            dst = recv.at[chunk, pl.ds(recv_base[s], size), :]
        else:
            d = stages - 1 - s
            b = order[d]
            at, size = region(my_l, order[:d + 1], rows)
            src = prob.at[pl.ds(pl.multiple_of(base + at, 8), size), :]
            dst = src
        return pltpu.make_async_remote_copy(
            src_ref=src, dst_ref=dst, send_sem=send_sem.at[s, chunk],
            recv_sem=recv_sem.at[s, chunk], device_id={"lmk": my_l ^ (1 << b)},
            device_id_type=pl.DeviceIdType.MESH)

    def finish(s, chunk):
        exchange(s, chunk).wait()
        if s < lbits:
            at, size = region(my_l, order[:s + 1], rows)
            here = pl.ds(pl.multiple_of(chunk * rows + at, 8), size)
            total = logit[here, :] + recv[chunk, pl.ds(recv_base[s], size), :]
            if s == lbits - 1:
                expo = jnp.exp(total - jnp.max(total, axis=1, keepdims=True))
                prob[here, :] = expo / jnp.sum(expo, axis=1, keepdims=True)
            else:
                logit[here, :] = total

    def forward(chunk):
        r = pl.ds(pl.multiple_of(chunk * rows, rows), rows)
        x = pts_ref[r, :]
        hi, lo = halves(x)
        ps[:, :feats] = hi
        ps[:, feats:2 * feats] = lo
        ps[:, 2 * feats:3 * feats] = hi
        norm = jnp.sum(x * x, axis=1, keepdims=True) * (-LOG2E / feats)
        ps[:, 3 * feats:] = extra_columns(norm, 0)
        total = None
        for j in range(m // tile):
            c = slice(j * tile, (j + 1) * tile)
            k = jnp.exp2(dot_nt(ps[...], ls[c, :]))
            hi, lo = halves(k)
            kh[r, c] = hi
            kl[r, c] = lo
            both = dot(hi, cc[c, :])
            term = both[:, :classes] + both[:, classes:] + dot(lo, cc[c, :classes])
            total = term if total is None else total + term
        logit[r, :] = total

    def backward(chunk):
        r = pl.ds(pl.multiple_of(chunk * rows, rows), rows)
        probs = prob[r, :].T
        labels = lab_ref[:, r]
        classes_at = lax.broadcasted_iota(jnp.int32, (classes, rows), 0)
        resid = probs - jnp.where(classes_at == labels, 1.0, 0.0)
        hi, lo = halves(resid)
        both = jnp.concatenate([hi, lo], axis=0)
        for j in range(m // tile):
            c = slice(j * tile, (j + 1) * tile)
            g = dot(both, kh[r, c])
            acc[:, c] += g[:classes] + g[classes:] + dot(hi, kl[r, c])

    start_back = max(chunks, stages + 1)

    def step(t, _):
        for s in range(stages, -1, -1):
            chunk = t - 1 - s

            @pl.when((chunk >= 0) & (chunk < chunks))
            def _():
                if s > 0:
                    finish(s - 1, chunk)
                if s < stages:
                    exchange(s, chunk).start()

        @pl.when(t < chunks)
        def _():
            forward(t)

        @pl.when(t >= start_back)
        def _():
            backward(t - start_back)

        return 0

    lax.fori_loop(0, start_back + chunks, step, 0)

    for j in range(m // tile):
        c = slice(j * tile, (j + 1) * tile)
        logit[c, :] = acc[:, c].T

    half = m // 2
    orders = [list(range(pbits)), list(range(pbits))[::-1]]
    gbase = [half - (half >> s) for s in range(pbits)]

    def gexchange(h, s):
        base = h * half
        if s < pbits:
            b = orders[h][s]
            at, size = region(my_p, orders[h][:s], half)
            size //= 2
            other = 1 - ((my_p >> b) & 1)
            src = logit.at[pl.ds(pl.multiple_of(base + at + other * size, 8), size), :]
            dst = grecv.at[h, pl.ds(gbase[s], size), :]
        else:
            d = 2 * pbits - 1 - s
            b = orders[h][d]
            at, size = region(my_p, orders[h][:d + 1], half)
            src = out_ref.at[pl.ds(pl.multiple_of(base + at, 8), size), :]
            dst = src
        return pltpu.make_async_remote_copy(
            src_ref=src, dst_ref=dst, send_sem=gsend.at[h, s],
            recv_sem=grecv_sem.at[h, s], device_id={"pts": my_p ^ (1 << b)},
            device_id_type=pl.DeviceIdType.MESH)

    for s in range(2 * pbits + 1):
        for h in range(2):
            if s > 0:
                gexchange(h, s - 1).wait()
                if s - 1 < pbits:
                    at, size = region(my_p, orders[h][:s], half)
                    here = pl.ds(pl.multiple_of(h * half + at, 8), size)
                    total = logit[here, :] + grecv[h, pl.ds(gbase[s - 1], size), :]
                    if s == pbits:
                        out_ref[here, :] = total * scale + RIDGE * coef_ref[here, :]
                    else:
                        logit[here, :] = total
            if s < 2 * pbits:
                gexchange(h, s).start()


def per_device(points, labels, landmarks, coefficients):
    npts, nlmk = lax.axis_size("pts"), lax.axis_size("lmk")
    n, feats = points.shape
    m, classes = coefficients.shape
    rows, tile = 512, 512
    chunks = n // rows
    wide = 3 * feats + 128
    stages = 2 * (nlmk.bit_length() - 1)
    gstages = 2 * (npts.bit_length() - 1)
    cfg = (rows, tile, npts, nlmk, LOSS_SCALE / (n * npts))
    vmem = pl.BlockSpec(memory_space=pltpu.VMEM)
    dma = pltpu.SemaphoreType.DMA
    return pl.pallas_call(
        functools.partial(body, cfg),
        out_shape=jax.ShapeDtypeStruct((m, classes), F32),
        in_specs=[vmem] * 4,
        out_specs=vmem,
        scratch_shapes=[
            pltpu.VMEM((m, wide), BF),
            pltpu.VMEM((m, 2 * classes), BF),
            pltpu.VMEM((rows, wide), BF),
            pltpu.VMEM((n, m), BF),
            pltpu.VMEM((n, m), BF),
            pltpu.VMEM((max(n, m), classes), F32),
            pltpu.VMEM((n, classes), F32),
            pltpu.VMEM((chunks, rows, classes), F32),
            pltpu.VMEM((classes, m), F32),
            pltpu.VMEM((2, m // 2, classes), F32),
            dma((stages, chunks)),
            dma((stages, chunks)),
            dma((2, gstages)),
            dma((2, gstages)),
        ],
        compiler_params=pltpu.CompilerParams(
            collective_id=0, has_side_effects=True, vmem_limit_bytes=67043328),
    )(points, labels.reshape(1, n), landmarks, coefficients)


def solution(mesh):
    in_specs = (P("pts", None), P("pts"), P("lmk", None), P("lmk", None))
    return jax.shard_map(
        per_device, mesh=mesh, in_specs=in_specs, out_specs=P("lmk", None), check_vma=False
    )
```

```python
import functools

import jax
import jax.numpy as jnp
from jax import lax
from jax.experimental import pallas as pl
from jax.experimental.pallas import tpu as pltpu
from jax.sharding import PartitionSpec as P

LOSS_SCALE = 8192.0
RIDGE = 0.5
LOG2E = 1.4426950408889634
BF = jnp.bfloat16
F32 = jnp.float32


def halves(x):
    hi = x.astype(BF)
    return hi, (x - hi.astype(F32)).astype(BF)


def dot(a, b):
    return jnp.dot(a, b, preferred_element_type=F32)


def dot_nt(a, b):
    return lax.dot_general(a, b, (((1,), (1,)), ((), ())), preferred_element_type=F32)


def extra_columns(norm, first):
    n1 = norm.astype(BF).astype(F32)
    n2 = (norm - n1).astype(BF).astype(F32)
    n3 = ((norm - n1) - n2).astype(BF).astype(F32)
    lane = lax.broadcasted_iota(jnp.int32, (norm.shape[0], 128), 1)
    ones = jnp.where((lane >= 3 - first) & (lane < 6 - first), 1.0, 0.0)
    ext = jnp.where(lane == first, n1, ones)
    ext = jnp.where(lane == first + 1, n2, ext)
    return jnp.where(lane == first + 2, n3, ext).astype(BF)


def body(cfg, pts_ref, lab_ref, lmk_ref, coef_ref, out_ref,
         ls, cc, ps, kh, kl, logit, prob, recv, acc, grecv,
         send_sem, recv_sem, gsend, grecv_sem):
    rows, tile, npts, nlmk, scale = cfg
    n, feats = pts_ref.shape
    m, classes = coef_ref.shape
    chunks = n // rows
    lbits, pbits = nlmk.bit_length() - 1, npts.bit_length() - 1
    stages = 2 * lbits
    my_l, my_p = lax.axis_index("lmk"), lax.axis_index("pts")

    barrier = pltpu.get_barrier_semaphore()
    for b in range(lbits):
        pl.semaphore_signal(barrier, inc=1, device_id={"lmk": my_l ^ (1 << b)},
                            device_id_type=pl.DeviceIdType.MESH)
    for b in range(pbits):
        pl.semaphore_signal(barrier, inc=1, device_id={"pts": my_p ^ (1 << b)},
                            device_id_type=pl.DeviceIdType.MESH)
    pl.semaphore_wait(barrier, lbits + pbits)

    def split_landmarks(i, _):
        r = pl.ds(pl.multiple_of(i * tile, tile), tile)
        x = lmk_ref[r, :]
        hi, lo = halves(x * (2.0 * LOG2E / feats))
        ls[r, :feats] = hi
        ls[r, feats:2 * feats] = hi
        ls[r, 2 * feats:3 * feats] = lo
        norm = jnp.sum(x * x, axis=1, keepdims=True) * (-LOG2E / feats)
        ls[r, 3 * feats:] = extra_columns(norm, 3)
        hi, lo = halves(coef_ref[r, :])
        cc[r, :classes] = hi
        cc[r, classes:] = lo
        return 0

    lax.fori_loop(0, m // tile, split_landmarks, 0)
    acc[...] = jnp.zeros_like(acc)

    def region(me, bits, total):
        offset, size = 0, total
        for b in bits:
            size //= 2
            offset = offset + ((me >> b) & 1) * size
        return offset, size

    order = list(range(lbits))
    recv_base = [rows - (rows >> s) for s in range(lbits)]

    def exchange(s, chunk):
        base = chunk * rows
        if s < lbits:
            b = order[s]
            at, size = region(my_l, order[:s], rows)
            size //= 2
            other = 1 - ((my_l >> b) & 1)
            src = logit.at[pl.ds(pl.multiple_of(base + at + other * size, 8), size), :]
            dst = recv.at[chunk, pl.ds(recv_base[s], size), :]
        else:
            d = stages - 1 - s
            b = order[d]
            at, size = region(my_l, order[:d + 1], rows)
            src = prob.at[pl.ds(pl.multiple_of(base + at, 8), size), :]
            dst = src
        return pltpu.make_async_remote_copy(
            src_ref=src, dst_ref=dst, send_sem=send_sem.at[s, chunk],
            recv_sem=recv_sem.at[s, chunk], device_id={"lmk": my_l ^ (1 << b)},
            device_id_type=pl.DeviceIdType.MESH)

    def finish(s, chunk):
        exchange(s, chunk).wait()
        if s < lbits:
            at, size = region(my_l, order[:s + 1], rows)
            here = pl.ds(pl.multiple_of(chunk * rows + at, 8), size)
            total = logit[here, :] + recv[chunk, pl.ds(recv_base[s], size), :]
            if s == lbits - 1:
                expo = jnp.exp(total - jnp.max(total, axis=1, keepdims=True))
                prob[here, :] = expo / jnp.sum(expo, axis=1, keepdims=True)
            else:
                logit[here, :] = total

    def split_points(chunk):
        r = pl.ds(pl.multiple_of(chunk * rows, rows), rows)
        x = pts_ref[r, :]
        hi, lo = halves(x)
        ps[:, :feats] = hi
        ps[:, feats:2 * feats] = lo
        ps[:, 2 * feats:3 * feats] = hi
        norm = jnp.sum(x * x, axis=1, keepdims=True) * (-LOG2E / feats)
        ps[:, 3 * feats:] = extra_columns(norm, 0)

    def forward(chunk, part):
        if part == 0:
            split_points(chunk)
        r = pl.ds(pl.multiple_of(chunk * rows, rows), rows)
        total = None if part == 0 else logit[r, :]
        tiles = m // tile
        for j in range(part * tiles // 2, (part + 1) * tiles // 2):
            c = slice(j * tile, (j + 1) * tile)
            k = jnp.exp2(dot_nt(ps[...], ls[c, :]))
            hi, lo = halves(k)
            kh[r, c] = hi
            kl[r, c] = lo
            both = dot(hi, cc[c, :])
            term = both[:, :classes] + both[:, classes:] + dot(lo, cc[c, :classes])
            total = term if total is None else total + term
        logit[r, :] = total

    def backward(chunk):
        r = pl.ds(pl.multiple_of(chunk * rows, rows), rows)
        probs = prob[r, :].T
        labels = lab_ref[:, r]
        classes_at = lax.broadcasted_iota(jnp.int32, (classes, rows), 0)
        resid = probs - jnp.where(classes_at == labels, 1.0, 0.0)
        hi, lo = halves(resid)
        both = jnp.concatenate([hi, lo], axis=0)
        for j in range(m // tile):
            c = slice(j * tile, (j + 1) * tile)
            g = dot(both, kh[r, c])
            acc[:, c] += g[:classes] + g[classes:] + dot(hi, kl[r, c])

    start_back = chunks + max(0, stages // 2 - (chunks - 1) // 2)

    def step(t, _):
        for part in range(2):
            for s in range(stages, -1, -1):
                if s % 2 != part:
                    continue
                chunk = t - 1 - s // 2

                @pl.when((chunk >= 0) & (chunk < chunks))
                def _():
                    if s > 0:
                        finish(s - 1, chunk)
                    if s < stages:
                        exchange(s, chunk).start()

            @pl.when(t < chunks)
            def _():
                forward(t, part)

            @pl.when(t >= start_back)
            def _():
                backward(2 * (t - start_back) + part)

        return 0

    lax.fori_loop(0, start_back + chunks // 2, step, 0)

    for j in range(m // tile):
        c = slice(j * tile, (j + 1) * tile)
        logit[c, :] = acc[:, c].T

    half = m // 2
    orders = [list(range(pbits)), list(range(pbits))[::-1]]
    gbase = [half - (half >> s) for s in range(pbits)]

    def gexchange(h, s):
        base = h * half
        if s < pbits:
            b = orders[h][s]
            at, size = region(my_p, orders[h][:s], half)
            size //= 2
            other = 1 - ((my_p >> b) & 1)
            src = logit.at[pl.ds(pl.multiple_of(base + at + other * size, 8), size), :]
            dst = grecv.at[h, pl.ds(gbase[s], size), :]
        else:
            d = 2 * pbits - 1 - s
            b = orders[h][d]
            at, size = region(my_p, orders[h][:d + 1], half)
            src = out_ref.at[pl.ds(pl.multiple_of(base + at, 8), size), :]
            dst = src
        return pltpu.make_async_remote_copy(
            src_ref=src, dst_ref=dst, send_sem=gsend.at[h, s],
            recv_sem=grecv_sem.at[h, s], device_id={"pts": my_p ^ (1 << b)},
            device_id_type=pl.DeviceIdType.MESH)

    for s in range(2 * pbits + 1):
        for h in range(2):
            if s > 0:
                gexchange(h, s - 1).wait()
                if s - 1 < pbits:
                    at, size = region(my_p, orders[h][:s], half)
                    here = pl.ds(pl.multiple_of(h * half + at, 8), size)
                    total = logit[here, :] + grecv[h, pl.ds(gbase[s - 1], size), :]
                    if s == pbits:
                        out_ref[here, :] = total * scale + RIDGE * coef_ref[here, :]
                    else:
                        logit[here, :] = total
            if s < 2 * pbits:
                gexchange(h, s).start()


def per_device(points, labels, landmarks, coefficients):
    npts, nlmk = lax.axis_size("pts"), lax.axis_size("lmk")
    n, feats = points.shape
    m, classes = coefficients.shape
    rows, tile = 512, 512
    chunks = n // rows
    wide = 3 * feats + 128
    stages = 2 * (nlmk.bit_length() - 1)
    gstages = 2 * (npts.bit_length() - 1)
    cfg = (rows, tile, npts, nlmk, LOSS_SCALE / (n * npts))
    vmem = pl.BlockSpec(memory_space=pltpu.VMEM)
    dma = pltpu.SemaphoreType.DMA
    return pl.pallas_call(
        functools.partial(body, cfg),
        out_shape=jax.ShapeDtypeStruct((m, classes), F32),
        in_specs=[vmem] * 4,
        out_specs=vmem,
        scratch_shapes=[
            pltpu.VMEM((m, wide), BF),
            pltpu.VMEM((m, 2 * classes), BF),
            pltpu.VMEM((rows, wide), BF),
            pltpu.VMEM((n, m), BF),
            pltpu.VMEM((n, m), BF),
            pltpu.VMEM((max(n, m), classes), F32),
            pltpu.VMEM((n, classes), F32),
            pltpu.VMEM((chunks, rows, classes), F32),
            pltpu.VMEM((classes, m), F32),
            pltpu.VMEM((2, m // 2, classes), F32),
            dma((stages, chunks)),
            dma((stages, chunks)),
            dma((2, gstages)),
            dma((2, gstages)),
        ],
        compiler_params=pltpu.CompilerParams(
            collective_id=0, has_side_effects=True, vmem_limit_bytes=67043328),
    )(points, labels.reshape(1, n), landmarks, coefficients)


def solution(mesh):
    in_specs = (P("pts", None), P("pts"), P("lmk", None), P("lmk", None))
    return jax.shard_map(
        per_device, mesh=mesh, in_specs=in_specs, out_specs=P("lmk", None), check_vma=False
    )
```
